128 devices in a mesh: gx: 32 (over y, x, core), gy: 4 (over z).
Axes of the slice: x: 4, y: 4, z: 4, core: 2. Of those that a mesh axis runs over, the one named last changes fastest.
Arguments:
- probes: float32 [16, 512, 128, 256], P(None, 'gx', 'gy'), may hold values from -6 to 6
- diffusivity: float32 [512, 128, 256], P('gx', 'gy'), may hold values from 0.5 to 2
- wind_speed: float32 [3], replicated, may hold values from 0.5 to 2
- sensor_cell: int32 [32, 4, 128], P('gx', 'gy'), may hold values from 0 to 131071
- sensor_owner: int32 [32, 4, 128, 1], P('gx', 'gy'), may hold values from 0 to 127; in each aligned block of 128 rows (0 to 127, 128 to 255, ..., all dimensions but the last counted through in order) at most 2 rows name the same one
- sensor_count: int32 [32, 4], P('gx', 'gy'), may hold values from 64 to 128
- goal_weight: float32 [32, 4, 128, 16], P('gx', 'gy'), may hold values from -0.6 to 0.6
Outputs:
- fields: float32 [16, 512, 128, 256], P(None, 'gx', 'gy')
- goal_block: float32 [2048, 16], P(('gx', 'gy'))
- ritz_gram: float32 [16, 16], replicated
The draws below stay inside these ranges and needn't reach their ends.
Inputs may be any that keep to these rules, and one draw needn't show every extreme that they name: `sensor_owner`: among the rows of one device, no owner is named more than 2 times, a bound that some block reaches.
All inputs are finite; a program needn't handle non-finite values.
Results may differ from the reference program's by a relative error of at most 0.0003.
Values sent between devices are 32-bit elements; how exact they have to be, the bound alone decides.
No kernel may reach another device: no remote copies, remote signals or barrier semaphores. Data moves between devices by JAX's collectives and lax.ppermute only.
A program may use at most 192 MiB of HBM per device.

```python
import math
import jax
import jax.numpy as jnp
import numpy as np
from jax import lax

CX = 16
CY = 32
CZ = 256
PROBES = 16
STEPS = 2
SWEEPS = 4
SENS = 128
CAP = 2
GOAL_DEV = 16
NX = 512
NY = 128
N_GX = 32
N_GY = 4


def place_ends(result, own_key, low, high):
    longest = result.shape.index(max(result.shape))
    spots = []
    for shift in (0, 1):
        where = [jax.random.randint(jax.random.fold_in(own_key, axis), (), 0, length) for axis, length in enumerate(result.shape)]
        where[longest] = (where[longest] + shift) % result.shape[longest]
        spots.append(tuple(where))
    return result.at[spots[0]].set(low).at[spots[1]].set(high)


def level_of(own_key, extent, cuts, least, high):
    def one(dim, parts):
        draws = jax.random.uniform(jax.random.fold_in(jax.random.fold_in(own_key, 6), dim), (parts,), jnp.float32, least / len(cuts), high / len(cuts))
        return jnp.repeat(jnp.exp(draws), extent[dim] // parts).reshape((-1,) + (1,) * (len(extent) - dim - 1))

    gain = one(*cuts[0])
    for cut in cuts[1:]:
        gain = gain * one(*cut)
    return gain


def shared_out(own_key, own, number, rows, count, top, bound, slope):
    ranking = jax.random.permutation(own_key, count)
    packed, common = shares(count, rows * top, bound, slope, True), shares(count, rows * top, bound, slope, False)
    places = jnp.arange(count)

    def named(lengths, turn):
        used = int((lengths > 0).sum())
        fixed = max(1, used // 4)
        shifted = fixed + (places - fixed + turn * (used - fixed)) % max(1, count - fixed)
        return jnp.zeros((count,), jnp.int32).at[ranking[jnp.where(places < fixed, places, shifted)]].set(jnp.asarray(lengths, jnp.int32))

    lengths = jnp.where(number % 4 == 0, named(packed, number // 4), named(common, number - number // 4 - 1))
    mixed = jax.random.permutation(jax.random.fold_in(own, 3), count)
    donor, sink = mixed[0:count // 2 * 2:2], mixed[1:count // 2 * 2:2]
    slack = jnp.minimum(lengths[donor] - 1, bound - lengths[sink]) // 2
    slack = jnp.where((donor == ranking[0]) | (sink == ranking[0]) | (lengths[sink] == 0), 0, jnp.maximum(slack, 0))
    shifted = jax.random.randint(jax.random.fold_in(own, 4), (count // 2,), 0, 1 << 20) % (slack + 1)
    lengths = lengths.at[donor].add(-shifted).at[sink].add(shifted)
    members = jnp.searchsorted(jnp.cumsum(lengths), jnp.arange(rows * top), side="right").astype(jnp.int32)
    table = members.reshape(top, rows).T
    table = table[jax.random.permutation(jax.random.fold_in(own, 1), rows)]
    turn = jax.random.randint(jax.random.fold_in(own, 2), (rows, 1), 0, top)
    return jnp.take_along_axis(table, (jnp.arange(top)[None, :] + turn) % top, axis=1)


def shares(number_of, total, limit, slope, full):
    weights = [(1 << 20) // math.isqrt(rank ** slope) + 1 for rank in range(1, number_of + 1)]
    largest = limit if full else min(limit, max(-(-total // number_of), total * weights[0] // sum(weights)))
    least = 1 if total - largest >= number_of - 1 else 0
    given, rest = [largest] + [least] * (number_of - 1), total - largest - least * (number_of - 1)
    while rest > 0:
        movable = [i for i in range(1, number_of) if given[i] < largest] or [i for i in range(1, number_of) if given[i] < limit]
        whole, left = sum([weights[i] for i in movable]), rest
        for i in movable:
            extra = min(limit - given[i], max(1, left * weights[i] // whole), rest)
            given[i] = given[i] + extra
            rest = rest - extra
    return np.array(given)


def centred(key, extent, spread, reach, cuts=(), held_as=jnp.bfloat16):
    level = level_of(key, extent, cuts, -0.22, 0.18) if cuts else 1.0
    entries = jax.random.normal(key, extent, jnp.float32) * spread * level
    return jnp.minimum(jnp.maximum(entries, -reach), reach).astype(held_as)


def setup_inputs(seed: int = 0) -> dict:
    arg_keys = jax.random.split(jax.random.key(seed), 8)
    probes = centred(arg_keys[0], (PROBES, NX, NY, CZ), 1.0, 6.0, ((1, 32), (2, 4)), jnp.float32)
    diffusivity = jnp.clip(jnp.exp(math.log(2.0) - 1.3862944 * jax.random.uniform(arg_keys[1], (NX, NY, CZ), jnp.float32) ** level_of(arg_keys[1], (NX, NY, CZ), ((0, 32), (1, 4)), -0.2, 0.2)), 0.5, 2.0)
    wind_speed = jnp.clip(jax.random.uniform(arg_keys[2], (3,), jnp.float32, 0.5, 2.0), 0.5, 2.0)
    sensor_cell = place_ends(jax.random.randint(arg_keys[3], (N_GX, N_GY, SENS), 0, CX * CY * CZ), jax.random.fold_in(arg_keys[3], 1), 0, (CX * CY * CZ) - 1).astype(jnp.int32)
    sensor_owner_keys = jax.random.split(jax.random.fold_in(arg_keys[4], 1), N_GX * N_GY * SENS // SENS)
    sensor_owner_turns = jax.random.permutation(jax.random.fold_in(arg_keys[4], 3), N_GX * N_GY * SENS // SENS)
    sensor_owner = jax.vmap(lambda own, number: shared_out(jax.random.fold_in(arg_keys[4], 2), own, number, SENS, N_GX * N_GY, 1, CAP, 1))(sensor_owner_keys, sensor_owner_turns).reshape((N_GX, N_GY, SENS, 1))
    sensor_count = place_ends(jax.random.randint(arg_keys[5], (N_GX, N_GY), SENS // 2, SENS + 1), jax.random.fold_in(arg_keys[5], 1), SENS // 2, SENS).astype(jnp.int32)
    goal_weight = centred(arg_keys[6], (N_GX, N_GY, SENS, GOAL_DEV), 0.1, 0.6, ((0, 32), (1, 4)), jnp.float32)
    return dict(probes=probes, diffusivity=diffusivity, wind_speed=wind_speed, sensor_cell=sensor_cell, sensor_owner=sensor_owner, sensor_count=sensor_count, goal_weight=goal_weight)


time_step = 2.0


def relax(padded, source, diffusion, wind_speed):
    centre = padded[..., 1:-1, 1:-1, :]
    widths = [(0, 0)] * (centre.ndim - 1) + [(1, 1)]
    zpadded = jnp.pad(centre, widths)
    beside = padded[..., 2:, 1:-1, :] + padded[..., :-2, 1:-1, :]
    beside = beside + padded[..., 1:-1, 2:, :] + padded[..., 1:-1, :-2, :]
    beside = beside + zpadded[..., 2:] + zpadded[..., :-2]
    upwind = wind_speed[0] * padded[..., :-2, 1:-1, :] + wind_speed[1] * padded[..., 1:-1, :-2, :] + wind_speed[2] * zpadded[..., :-2]
    diagonal = 1.0 + time_step * (6.0 * diffusion + wind_speed[0] + wind_speed[1] + wind_speed[2])
    updated = (source + time_step * (diffusion * beside + upwind)) / diagonal
    return jnp.where(diffusion > 0.0, updated, 0.0)


def reference(probes, diffusivity, wind_speed, sensor_cell, sensor_owner, sensor_count, goal_weight):
    def advance(state_field):
        for step_index in range(STEPS):
            source = state_field
            for sweep_index in range(SWEEPS):
                state_field = relax(jnp.pad(state_field, ((1, 1), (1, 1), (0, 0))), source, diffusivity, wind_speed)
        return state_field

    fields = lax.map(advance, probes)
    blocks = fields.reshape(PROBES, N_GX, CX, N_GY, CY, CZ).transpose(1, 3, 0, 2, 4, 5)
    blocks = blocks.reshape(N_GX, N_GY, PROBES, CX * CY * CZ)
    readings = jnp.take_along_axis(blocks, sensor_cell[:, :, None, :].astype(jnp.int32), axis=3)
    active = (jnp.arange(SENS, dtype=jnp.int32)[None, None, :] < sensor_count[:, :, None]).astype(jnp.float32)
    readings = readings.transpose(0, 1, 3, 2) * active[..., None]
    outer = (goal_weight[..., :, None] * readings[..., None, :]).reshape(N_GX * N_GY * SENS, GOAL_DEV * PROBES)
    owners = sensor_owner.reshape(-1)
    onehot = (owners[:, None] == jnp.arange(N_GX * N_GY, dtype=jnp.int32)[None, :]).astype(jnp.float32)
    goal_block = jnp.dot(onehot.T, outer, precision=lax.Precision.HIGHEST).reshape(N_GX * N_GY * GOAL_DEV, PROBES)
    ritz_gram = jnp.dot(goal_block.T, goal_block, precision=lax.Precision.HIGHEST)
    return fields, goal_block, ritz_gram
```

```python
import functools

import jax
import jax.numpy as jnp
from jax import lax
from jax.experimental import pallas as pl
from jax.experimental.pallas import tpu as pltpu
from jax.sharding import Mesh
from jax.sharding import PartitionSpec as P

SWEEPS = 4
H = SWEEPS
ALL = ("gx_0", "gx_1", "gx_2", "gy")
GX = ("gx_0", "gx_1", "gx_2")
G = 8
TAU = 2.0
F32 = jnp.float32
ANY = pl.BlockSpec(memory_space=pl.ANY)
SMEM = pl.BlockSpec(memory_space=pltpu.SMEM)
VMEM = pl.BlockSpec(memory_space=pltpu.VMEM)
DMA = pltpu.SemaphoreType.DMA
NX, NY, NZ = 16, 32, 256
TILES = NY // 8


def both(pairs):
    return pairs + [(b, a) for a, b in pairs]


def near(x):
    return pltpu.with_memory_space_constraint(x, pltpu.VMEM)


def kernel(body, name, operands, outs, scratch, in_specs, microseconds, mib, aliases=None):
    placed = [near(x) if spec is VMEM else x for x, spec in zip(operands, in_specs)]
    out_shape = [pltpu.VMEM(dims, F32) if spec is VMEM else jax.ShapeDtypeStruct(dims, F32) for dims, spec in outs]
    return pl.pallas_call(
        body,
        in_specs=in_specs,
        out_specs=[spec for _, spec in outs],
        out_shape=out_shape,
        scratch_shapes=scratch,
        input_output_aliases=aliases or {},
        compiler_params=pltpu.CompilerParams(vmem_limit_bytes=mib * 1024 * 1024),
        cost_estimate=pl.CostEstimate(flops=0, transcendentals=0, bytes_accessed=int(microseconds * 3.5e6)),
        name=name,
    )(*placed)


def sorting(inverse):
    row = lax.broadcasted_iota(jnp.int32, (NZ, NZ), 0)
    col = lax.broadcasted_iota(jnp.int32, (NZ, NZ), 1)
    if inverse:
        row, col = col, row
    source = jnp.where(col < NZ // 2, 2 * col, 2 * col - (NZ - 1))
    return (row == source).astype(F32).astype(jnp.bfloat16)


def reorder(v, matrix):
    high = v.astype(jnp.bfloat16)
    rest = v - high.astype(F32)
    mid = rest.astype(jnp.bfloat16)
    low = (rest - mid.astype(F32)).astype(jnp.bfloat16)
    dot = functools.partial(jnp.dot, preferred_element_type=F32)
    return dot(high, matrix) + (dot(mid, matrix) + dot(low, matrix))


def copy_all(pairs, sems):
    made = [pltpu.make_async_copy(a, b, sems.at[i]) for i, (a, b) in enumerate(pairs)]
    for c in made:
        c.start()
    for c in made:
        c.wait()


def face_pairs(field, place, x0, y0, b_out, c_out, d_out):
    return [
        (field.at[pl.ds(x0 + place[0], H), pl.ds(y0, NY)], b_out.at[:, pl.ds(0, NY)]),
        (field.at[pl.ds(x0, NX), pl.ds(y0 + place[2], H)], c_out.at[:, pl.ds(0, H)]),
        (field.at[pl.ds(x0, NX), pl.ds(y0 + place[3], H)], d_out.at[:, pl.ds(0, H)]),
    ]


def face_outs(extra):
    more = 1 if extra else 0
    faces = [(H, NY + TILES * more, G, NZ), (NX, H + more, G, NZ), (NX, H + more, G, NZ)]
    return [(dims, VMEM) for dims in faces]


PLANES = 4


def pack_kernel(g, place, probes, *rest):
    a_in = rest[0] if g == 0 else None
    s_out, b_out, c_out, d_out, raw, mat, sem_in, sem_f = rest[-8:]

    def load(i):
        src = probes.at[pl.ds(g * G, G), pl.ds(i * PLANES, PLANES)]
        return pltpu.make_async_copy(src, raw.at[:, pl.ds(i * PLANES, PLANES)], sem_in.at[i])

    for i in range(NX // PLANES):
        load(i).start()
    mat[...] = sorting(False)

    def planes(i, carry):
        load(i).wait()
        rows = [jnp.swapaxes(raw[:, i * PLANES + k], 0, 1).reshape(NY * G, NZ) for k in range(PLANES)]
        rows = reorder(jnp.concatenate(rows, axis=0), mat[...])
        s_out[pl.ds(i * PLANES, PLANES)] = rows.reshape(PLANES, NY, G, NZ)
        return carry

    lax.fori_loop(0, NX // PLANES, planes, 0)
    pairs = face_pairs(s_out, place, 0, 0, b_out, c_out, d_out)
    if g == 0:
        pairs += [
            (a_in.at[pl.ds(place[0], H)], b_out.at[:, pl.ds(NY, TILES)]),
            (a_in.at[:, pl.ds(place[10], 1)], c_out.at[:, pl.ds(H, 1)]),
            (a_in.at[:, pl.ds(place[11], 1)], d_out.at[:, pl.ds(H, 1)]),
        ]
    copy_all(pairs, sem_f)


def pack(g, place, probes, a):
    more = [a] if g == 0 else []
    return kernel(
        functools.partial(pack_kernel, g),
        f"pack{g}",
        [place, probes] + more,
        [((NX, NY, G, NZ), VMEM)] + face_outs(g == 0),
        [
            pltpu.VMEM((G, NX, NY, NZ), F32),
            pltpu.VMEM((NZ, NZ), jnp.bfloat16),
            DMA((NX // PLANES,)),
            DMA((6,)),
        ],
        [SMEM, ANY] + [VMEM] * len(more),
        6,
        12,
    )


def corner_kernel(place, field, c_in, d_in, *rest):
    a_out, e_out, sems = rest[-3:]
    inner, outer = pl.ds(place[1], H), pl.ds(place[0], H)
    rows = pl.ds(0, H)
    pairs = [
        (field.at[inner], a_out.at[:, pl.ds(H, NY)]),
        (c_in.at[inner, rows], a_out.at[:, pl.ds(place[4], H)]),
        (d_in.at[inner, rows], a_out.at[:, pl.ds(place[5], H)]),
        (c_in.at[outer, rows], e_out.at[:, pl.ds(place[6], H)]),
        (d_in.at[outer, rows], e_out.at[:, pl.ds(place[7], H)]),
    ]
    if len(rest) > 3:
        tile, base = pl.ds(H, 1), NY + 2 * H
        pairs += [
            (rest[0].at[inner], a_out.at[:, pl.ds(base + 1, TILES)]),
            (c_in.at[inner, tile], a_out.at[:, pl.ds(base + place[12], 1)]),
            (d_in.at[inner, tile], a_out.at[:, pl.ds(base + place[13], 1)]),
            (c_in.at[outer, tile], e_out.at[:, pl.ds(2 * H + place[14], 1)]),
            (d_in.at[outer, tile], e_out.at[:, pl.ds(2 * H + place[15], 1)]),
        ]
    copy_all(pairs, sems)


def corners(place, field, c_in, d_in, a=None):
    more = [] if a is None else [a]
    n = len(more)
    return kernel(
        corner_kernel,
        "corners",
        [place, field, c_in, d_in] + more,
        [((H, NY + 2 * H + (TILES + 2) * n, G, NZ), VMEM), ((H, 2 * H + 2 * n, G, NZ), VMEM)],
        [DMA((10,))],
        [SMEM] + [VMEM] * (3 + n),
        1,
        2,
    )


def coefficient_kernel(place, wind, a_own, a_in, b_in, c_in, d_in, e_in, out, wide, mat, sems):
    base = NY + 2 * H
    outer, own, tile = pl.ds(place[8], H), pl.ds(1, TILES), pl.ds(H, 1)
    copy_all(
        [
            (a_own, wide.at[pl.ds(H, NX), own]),
            (a_in.at[:, pl.ds(base, TILES + 2)], wide.at[pl.ds(place[9], H)]),
            (b_in.at[:, pl.ds(NY, TILES)], wide.at[outer, own]),
            (c_in.at[:, tile], wide.at[pl.ds(H, NX), pl.ds(place[12], 1)]),
            (d_in.at[:, tile], wide.at[pl.ds(H, NX), pl.ds(place[13], 1)]),
            (e_in.at[:, pl.ds(2 * H, 1)], wide.at[outer, pl.ds(0, 1)]),
            (e_in.at[:, pl.ds(2 * H + 1, 1)], wide.at[outer, pl.ds(TILES + 1, 1)]),
        ],
        sems,
    )
    mat[...] = sorting(False)
    w = [wind[i] for i in range(3)]
    count = 8 * (TILES + 2)

    def planes(i, carry):
        x = pl.ds(i * H, H)
        a = reorder(wide[x].reshape(H * count, NZ), mat[...])
        inverse = 1.0 / (1.0 + TAU * (6.0 * a + (w[0] + w[1] + w[2])))
        inverse = jnp.where(a > 0.0, inverse, 0.0)
        spread = TAU * a * inverse
        lane = lax.broadcasted_iota(jnp.int32, a.shape, 1)
        parts = [
            spread,
            spread + (TAU * w[0]) * inverse,
            spread + (TAU * w[1]) * inverse,
            jnp.where(lane == 0, 0.0, spread + (TAU * w[2]) * inverse),
            inverse,
        ]
        for k, part in enumerate(parts):
            out[k, x] = part.reshape(H, count, NZ)
        return carry

    lax.fori_loop(0, (NX + 2 * H) // H, planes, 0)


def coefficients(place, wind, a_own, state):
    wide = (NX + 2 * H, TILES + 2, 8, NZ)
    return kernel(
        coefficient_kernel,
        "coefficients",
        [place, wind, a_own] + state[1:6],
        [((5, NX + 2 * H, 8 * (TILES + 2), NZ), VMEM)],
        [pltpu.VMEM(wide, F32), pltpu.VMEM((NZ, NZ), jnp.bfloat16), DMA((7,))],
        [SMEM, SMEM] + [VMEM] * 6,
        3,
        6,
    )[0]


SHIFT = 8 - H


def sweep(number, src, dst, scaled, coef):
    nx, ny = src.shape[:2]
    last = lax.broadcasted_iota(jnp.int32, (G, 128), 1) == 127
    block = 2

    def row(ref, x, y, z):
        return ref[x, y, :, z * 128 : (z + 1) * 128]

    def rows(ref, x, y):
        return [row(ref, x, y, z) for z in (0, 1)]

    def spread(k, x, y, z):
        y = y + SHIFT
        return jnp.broadcast_to(coef[k, x, y : y + 1, z * 128 : (z + 1) * 128], (G, 128))

    def planes(i, carry):
        xs = [number + block * i + k for k in range(block)]
        below = [rows(src, x, number - 1) for x in xs]
        here = [rows(src, x, number) for x in xs]
        for y in range(number, ny - number):
            above = [rows(src, x, y + 1) for x in xs]
            beside = [rows(src, xs[0] - 1, y)] + here + [rows(src, xs[-1] + 1, y)]
            for k, x in enumerate(xs):
                even, odd = here[k]
                up = [odd, jnp.where(last, 0.0, pltpu.roll(even, 127, 1))]
                down = [pltpu.roll(odd, 1, 1), even]
                for z in (0, 1):
                    if number == 1:
                        part = here[k][z] * spread(4, x, y, z)
                        scaled[x, y, :, z * 128 : (z + 1) * 128] = part
                    else:
                        part = row(scaled, x, y, z)
                    part = part + spread(0, x, y, z) * (beside[k + 2][z] + (above[k][z] + up[z]))
                    other = spread(1, x, y, z) * beside[k][z] + spread(2, x, y, z) * below[k][z]
                    dst[x, y, :, z * 128 : (z + 1) * 128] = (part + spread(3, x, y, z) * down[z]) + other
            below, here = here, above
        return carry

    lax.fori_loop(0, (nx - 2 * number) // block, planes, 0)


def gather_state(place, field, a_in, b_in, c_in, d_in, e_in, u, sems):
    outer, own_x, own_y, rows = pl.ds(place[8], H), pl.ds(H, NX), pl.ds(H, NY), pl.ds(0, H)
    copy_all(
        [
            (field, u.at[own_x, own_y]),
            (a_in.at[:, pl.ds(0, NY + 2 * H)], u.at[pl.ds(place[9], H)]),
            (b_in.at[:, pl.ds(0, NY)], u.at[outer, own_y]),
            (c_in.at[:, rows], u.at[own_x, pl.ds(place[4], H)]),
            (d_in.at[:, rows], u.at[own_x, pl.ds(place[5], H)]),
            (e_in.at[:, rows], u.at[outer, rows]),
            (e_in.at[:, pl.ds(H, H)], u.at[outer, pl.ds(H + NY, H)]),
        ],
        sems,
    )


def sweeps(u, v, scaled, coef):
    for number in range(1, SWEEPS + 1):
        sweep(number, u, v, scaled, coef)
        u, v = v, u


def step_kernel(place, field, a_in, b_in, c_in, d_in, e_in, coef, s_out, b_out, c_out, d_out, u, v, scaled, sems):
    gather_state(place, field, a_in, b_in, c_in, d_in, e_in, u, sems)
    sweeps(u, v, scaled, coef)
    own = u.at[pl.ds(H, NX), pl.ds(H, NY)]
    copy_all(face_pairs(u, place, H, H, b_out, c_out, d_out) + [(own, s_out)], sems)


STATE_SCRATCH = [pltpu.VMEM((NX + 2 * H, NY + 2 * H, G, NZ), F32)] * 3


def step(g, place, state):
    return kernel(
        step_kernel,
        f"step{g}",
        [place, *state],
        [((NX, NY, G, NZ), VMEM)] + face_outs(False),
        STATE_SCRATCH + [DMA((8,))],
        [SMEM] + [VMEM] * 7,
        12,
        24,
    )


def read_sensors(cells, u, out):
    lane = lax.broadcasted_iota(jnp.int32, (G, 128), 1)

    def one(s, found):
        cell = cells[s]
        x, y, z = cell // (NY * NZ), (cell // NZ) % NY, cell % NZ
        half = pl.multiple_of((z % 2) * 128, 128)
        value = pltpu.roll(u[x + H, y + H, :, pl.ds(half, 128)], (s - z // 2 + 128) % 128, 1)
        return jnp.where(lane == s, value, found)

    out[...] = lax.fori_loop(0, 128, one, jnp.zeros((G, 128), F32), unroll=8)


def last_kernel(g, place, cells, field, a_in, b_in, c_in, d_in, e_in, coef, *rest):
    out, reading, u, v, scaled, stage, mat, sems, sem_out = rest[-9:]
    gather_state(place, field, a_in, b_in, c_in, d_in, e_in, u, sems)
    mat[...] = sorting(True)
    sweeps(u, v, scaled, coef)

    def store(i):
        dst = out.at[pl.ds(g * G, G), pl.ds(i * PLANES, PLANES)]
        return pltpu.make_async_copy(stage.at[:, pl.ds(i * PLANES, PLANES)], dst, sem_out.at[i])

    def planes(i, carry):
        rows = u[pl.ds(i * PLANES + H, PLANES), pl.ds(H, NY)].reshape(PLANES * NY * G, NZ)
        rows = reorder(rows, mat[...]).reshape(PLANES, NY, G, NZ)
        for k in range(PLANES):
            stage[:, i * PLANES + k] = jnp.swapaxes(rows[k], 0, 1)
        store(i).start()
        return carry

    lax.fori_loop(0, NX // PLANES, planes, 0)
    read_sensors(cells, u, reading)
    for i in range(NX // PLANES):
        store(i).wait()


def last_step(g, place, cells, state, fields=None):
    more = [] if fields is None else [fields]
    return kernel(
        functools.partial(last_kernel, g),
        f"last{g}",
        [place, cells, *state] + more,
        [((2 * G, NX, NY, NZ), ANY), ((G, 128), VMEM)],
        STATE_SCRATCH
        + [
            pltpu.VMEM((G, NX, NY, NZ), F32),
            pltpu.VMEM((NZ, NZ), jnp.bfloat16),
            DMA((8,)),
            DMA((NX // PLANES,)),
        ],
        [SMEM, SMEM] + [VMEM] * 7 + [ANY] * len(more),
        16,
        30,
        {9: 0} if more else {},
    )


def readings_exchange(readings, sensor_owner, sensor_count, goal_weight):
    probe_count, sensor_rows = readings.shape
    goal_count = goal_weight.shape[3]
    device_count = lax.axis_size(ALL)
    capacity = max(2, (sensor_rows + device_count - 1) // device_count)
    row_index = jnp.arange(sensor_rows, dtype=jnp.int32)
    active = (row_index < sensor_count.reshape(())).astype(F32)
    readings = readings.T * active[:, None]
    weights = goal_weight.reshape(sensor_rows, goal_count)
    owners = sensor_owner.reshape(sensor_rows)
    earlier = (owners[None, :] == owners[:, None]) & (row_index[None, :] < row_index[:, None])
    slot_rank = jnp.sum(earlier.astype(jnp.int32), axis=1)
    slot_index = owners * capacity + slot_rank
    slots = jnp.arange(device_count * capacity, dtype=jnp.int32)
    placing = (slots[:, None] == slot_index[None, :]).astype(F32)
    payload = jnp.concatenate([readings, weights], axis=1)
    outgoing = jnp.dot(placing, payload, precision=lax.Precision.HIGHEST)
    outgoing = outgoing.reshape(device_count, capacity, probe_count + goal_count)
    received = lax.all_to_all(outgoing, ALL, split_axis=0, concat_axis=0, tiled=True)
    received = received.reshape(device_count * capacity, probe_count + goal_count)
    goal_block = jnp.dot(
        received[:, probe_count:].T, received[:, :probe_count], precision=lax.Precision.HIGHEST
    )
    own = jnp.dot(goal_block.T, goal_block, precision=lax.Precision.HIGHEST)
    terms = jnp.broadcast_to(own.reshape(1, -1), (device_count, own.size))
    terms = lax.all_to_all(terms, ALL, split_axis=0, concat_axis=0, tiled=True)
    return goal_block, jnp.sum(terms, axis=0).reshape(own.shape)


def body(probes, diffusivity, wind_speed, sensor_cell, sensor_owner, sensor_count, goal_weight):
    core = lax.axis_index("gx_2")
    odd = lax.axis_index("gy") % 2

    def either(flag, zero, one):
        return jnp.where(flag == 0, zero, one)

    place = jnp.stack(
        [
            either(core, 0, NX - H),
            either(core, NX - H, 0),
            either(odd, NY - H, 0),
            either(odd, 0, NY - H),
            either(odd, NY + H, 0),
            either(odd, 0, NY + H),
            either(odd, H, 0),
            either(odd, 0, H),
            either(core, 0, NX + H),
            either(core, NX + H, 0),
            either(odd, TILES - 1, 0),
            either(odd, 0, TILES - 1),
            either(odd, TILES + 1, 0),
            either(odd, 0, TILES + 1),
            either(odd, 1, 0),
            either(odd, 0, 1),
        ]
    ).astype(jnp.int32)
    peers_x, peers_y = lax.axis_size(GX), lax.axis_size("gy")
    inner = both([(i, i + 1) for i in range(0, peers_x - 1, 2)])
    outer = both([(i, i + 1) for i in range(1, peers_x - 1, 2)])
    first = both([(i, i + 1) for i in range(0, peers_y - 1, 2)])
    second = both([(i, i + 1) for i in range(1, peers_y - 1, 2)])

    def rows(c, d):
        return lax.ppermute(c, "gy", first), lax.ppermute(d, "gy", second)

    def planes(b):
        return lax.ppermute(b, GX, outer)

    def after(values, others):
        return lax.optimization_barrier((tuple(values), tuple(others)))[0]

    def finish(field, c, d, own=None):
        a, e = corners(place, field, c, d, own)
        return lax.ppermute(a, GX, inner), lax.ppermute(e, GX, outer), (a, e)

    probes = pltpu.with_memory_space_constraint(probes, pltpu.HBM)
    a_own = diffusivity.reshape(NX, TILES, 8, NZ)
    cells = sensor_cell.reshape(-1)
    made = [pack(0, place, probes, a_own), pack(1, place, probes, a_own)]
    c, d = rows(*made[0][2:])
    b = planes(made[0][1])
    c, d, b, *made[1] = after((c, d, b, *made[1]), ())
    coef = fields = None
    readings = []
    for turn in range(4):
        g, field = turn % 2, made[turn][0]
        a, e, sent = finish(field, c, d, a_own if turn == 0 else None)
        state = [field, a, b, c, d, e]
        if turn < 3:
            c, d = rows(*after(made[turn + 1][2:], sent))
            b = planes(*after(made[turn + 1][1:2], (e,)))
        if turn == 0:
            coef = coefficients(place, wind_speed, a_own, state)
        if turn < 2:
            c, d, b, *out = after((c, d, b, *step(g, place, state + [coef])), ())
            made.append(out)
        else:
            fields, reading = last_step(g, place, cells, state + [coef], fields)
            readings.append(reading)
            if turn == 2:
                c, d, b, fields = after((c, d, b, fields), ())
    readings = jnp.concatenate(readings, axis=0)
    goal_block, ritz_gram = readings_exchange(readings, sensor_owner, sensor_count, goal_weight)
    return fields, goal_block, ritz_gram


def solution(mesh):
    torus = Mesh(mesh.devices.reshape(4, 4, 2, mesh.shape["gy"]), ALL)
    return jax.shard_map(
        body,
        mesh=torus,
        in_specs=(
            P(None, GX, "gy", None),
            P(GX, "gy", None),
            P(),
            P(GX, "gy", None),
            P(GX, "gy", None, None),
            P(GX, "gy"),
            P(GX, "gy", None, None),
        ),
        out_specs=(P(None, GX, "gy", None), P(ALL, None), P()),
        check_vma=False,
    )
```

```python
import functools

import jax
import jax.numpy as jnp
from jax import lax
from jax.experimental import pallas as pl
from jax.experimental.pallas import tpu as pltpu
from jax.sharding import Mesh
from jax.sharding import PartitionSpec as P

SWEEPS = 4
H = SWEEPS
ALL = ("gx_0", "gx_1", "gx_2", "gy")
GX = ("gx_0", "gx_1", "gx_2")
G = 8
TAU = 2.0
F32 = jnp.float32
ANY = pl.BlockSpec(memory_space=pl.ANY)
SMEM = pl.BlockSpec(memory_space=pltpu.SMEM)
VMEM = pl.BlockSpec(memory_space=pltpu.VMEM)
DMA = pltpu.SemaphoreType.DMA
NX, NY, NZ = 16, 32, 256
TILES = NY // 8


def both(pairs):
    return pairs + [(b, a) for a, b in pairs]


def near(x):
    return pltpu.with_memory_space_constraint(x, pltpu.VMEM)


def kernel(body, name, operands, outs, scratch, in_specs, microseconds, mib, aliases=None):
    placed = [near(x) if spec is VMEM else x for x, spec in zip(operands, in_specs)]
    out_shape = [pltpu.VMEM(dims, F32) if spec is VMEM else jax.ShapeDtypeStruct(dims, F32) for dims, spec in outs]
    return pl.pallas_call(
        body,
        in_specs=in_specs,
        out_specs=[spec for _, spec in outs],
        out_shape=out_shape,
        scratch_shapes=scratch,
        input_output_aliases=aliases or {},
        compiler_params=pltpu.CompilerParams(vmem_limit_bytes=mib * 1024 * 1024),
        cost_estimate=pl.CostEstimate(flops=0, transcendentals=0, bytes_accessed=int(microseconds * 3.5e6)),
        name=name,
    )(*placed)


def sorting(inverse):
    row = lax.broadcasted_iota(jnp.int32, (NZ, NZ), 0)
    col = lax.broadcasted_iota(jnp.int32, (NZ, NZ), 1)
    if inverse:
        row, col = col, row
    source = jnp.where(col < NZ // 2, 2 * col, 2 * col - (NZ - 1))
    return (row == source).astype(F32).astype(jnp.bfloat16)


def reorder(v, matrix):
    high = v.astype(jnp.bfloat16)
    rest = v - high.astype(F32)
    mid = rest.astype(jnp.bfloat16)
    low = (rest - mid.astype(F32)).astype(jnp.bfloat16)
    dot = functools.partial(jnp.dot, preferred_element_type=F32)
    return dot(high, matrix) + (dot(mid, matrix) + dot(low, matrix))


def copy_all(pairs, sems):
    made = [pltpu.make_async_copy(a, b, sems.at[i]) for i, (a, b) in enumerate(pairs)]
    for c in made:
        c.start()
    for c in made:
        c.wait()


def face_pairs(field, place, x0, y0, outs):
    planes, all_x, all_y = pl.ds(x0 + place[0], H), pl.ds(x0, NX), pl.ds(y0, NY)
    c_rows, d_rows = pl.ds(y0 + place[2], H), pl.ds(y0 + place[3], H)
    taken = [(planes, all_y), (all_x, c_rows), (all_x, d_rows), (planes, c_rows), (planes, d_rows)]
    return [(field.at[x, y], out.at[:, pl.ds(0, NY if y is all_y else H)]) for (x, y), out in zip(taken, outs)]


def face_outs(extra):
    more = 1 if extra else 0
    faces = [(H, NY + TILES * more, G, NZ)] + [(NX, H + more, G, NZ)] * 2 + [(H, H + more, G, NZ)] * 2
    return [(dims, VMEM) for dims in faces]


PLANES = 4


def pack_kernel(g, place, probes, *rest):
    a_in = rest[0] if g == 0 else None
    s_out, *outs = rest[-10:-4]
    raw, mat, sem_in, sem_f = rest[-4:]

    def load(i):
        src = probes.at[pl.ds(g * G, G), pl.ds(i * PLANES, PLANES)]
        return pltpu.make_async_copy(src, raw.at[:, pl.ds(i * PLANES, PLANES)], sem_in.at[i])

    for i in range(NX // PLANES):
        load(i).start()
    mat[...] = sorting(False)

    def planes(i, carry):
        load(i).wait()
        rows = [jnp.swapaxes(raw[:, i * PLANES + k], 0, 1).reshape(NY * G, NZ) for k in range(PLANES)]
        rows = reorder(jnp.concatenate(rows, axis=0), mat[...])
        s_out[pl.ds(i * PLANES, PLANES)] = rows.reshape(PLANES, NY, G, NZ)
        return carry

    lax.fori_loop(0, NX // PLANES, planes, 0)
    pairs = face_pairs(s_out, place, 0, 0, outs)
    if g == 0:
        planes_out, c_tile, d_tile = pl.ds(place[0], H), pl.ds(place[10], 1), pl.ds(place[11], 1)
        pairs += [
            (a_in.at[planes_out], outs[0].at[:, pl.ds(NY, TILES)]),
            (a_in.at[:, c_tile], outs[1].at[:, pl.ds(H, 1)]),
            (a_in.at[:, d_tile], outs[2].at[:, pl.ds(H, 1)]),
            (a_in.at[planes_out, c_tile], outs[3].at[:, pl.ds(H, 1)]),
            (a_in.at[planes_out, d_tile], outs[4].at[:, pl.ds(H, 1)]),
        ]
    copy_all(pairs, sem_f)


def pack(g, place, probes, a):
    more = [a] if g == 0 else []
    return kernel(
        functools.partial(pack_kernel, g),
        f"pack{g}",
        [place, probes] + more,
        [((NX, NY, G, NZ), VMEM)] + face_outs(g == 0),
        [
            pltpu.VMEM((G, NX, NY, NZ), F32),
            pltpu.VMEM((NZ, NZ), jnp.bfloat16),
            DMA((NX // PLANES,)),
            DMA((10,)),
        ],
        [SMEM, ANY] + [VMEM] * len(more),
        6,
        12,
    )


def inner_kernel(place, field, c_in, d_in, *rest):
    out, sems = rest[-2:]
    inner, rows = pl.ds(place[1], H), pl.ds(0, H)
    pairs = [
        (field.at[inner], out.at[:, pl.ds(H, NY)]),
        (c_in.at[inner, rows], out.at[:, pl.ds(place[4], H)]),
        (d_in.at[inner, rows], out.at[:, pl.ds(place[5], H)]),
    ]
    if len(rest) > 2:
        tile, base = pl.ds(H, 1), NY + 2 * H
        pairs += [
            (rest[0].at[inner], out.at[:, pl.ds(base + 1, TILES)]),
            (c_in.at[inner, tile], out.at[:, pl.ds(base + place[12], 1)]),
            (d_in.at[inner, tile], out.at[:, pl.ds(base + place[13], 1)]),
        ]
    copy_all(pairs, sems)


def inner_planes(place, field, c_in, d_in, a=None):
    more = [] if a is None else [a]
    n = len(more)
    return kernel(
        inner_kernel,
        "inner",
        [place, field, c_in, d_in] + more,
        [((H, NY + 2 * H + (TILES + 2) * n, G, NZ), VMEM)],
        [DMA((6,))],
        [SMEM] + [VMEM] * (3 + n),
        1,
        2,
    )[0]


def coefficient_kernel(place, wind, a_own, a_in, b_in, c_in, d_in, f_in, h_in, out, wide, mat, sems):
    base = NY + 2 * H
    outer, own, tile = pl.ds(place[8], H), pl.ds(1, TILES), pl.ds(H, 1)
    copy_all(
        [
            (a_own, wide.at[pl.ds(H, NX), own]),
            (a_in.at[:, pl.ds(base, TILES + 2)], wide.at[pl.ds(place[9], H)]),
            (b_in.at[:, pl.ds(NY, TILES)], wide.at[outer, own]),
            (c_in.at[:, tile], wide.at[pl.ds(H, NX), pl.ds(place[12], 1)]),
            (d_in.at[:, tile], wide.at[pl.ds(H, NX), pl.ds(place[13], 1)]),
            (f_in.at[:, tile], wide.at[outer, pl.ds(place[12], 1)]),
            (h_in.at[:, tile], wide.at[outer, pl.ds(place[13], 1)]),
        ],
        sems,
    )
    mat[...] = sorting(False)
    w = [wind[i] for i in range(3)]
    count = 8 * (TILES + 2)

    def planes(i, carry):
        x = pl.ds(i * H, H)
        a = reorder(wide[x].reshape(H * count, NZ), mat[...])
        inverse = 1.0 / (1.0 + TAU * (6.0 * a + (w[0] + w[1] + w[2])))
        inverse = jnp.where(a > 0.0, inverse, 0.0)
        spread = TAU * a * inverse
        lane = lax.broadcasted_iota(jnp.int32, a.shape, 1)
        parts = [
            spread,
            spread + (TAU * w[0]) * inverse,
            spread + (TAU * w[1]) * inverse,
            jnp.where(lane == 0, 0.0, spread + (TAU * w[2]) * inverse),
            inverse,
        ]
        for k, part in enumerate(parts):
            out[k, x] = part.reshape(H, count, NZ)
        return carry

    lax.fori_loop(0, (NX + 2 * H) // H, planes, 0)


def coefficients(place, wind, a_own, state):
    wide = (NX + 2 * H, TILES + 2, 8, NZ)
    return kernel(
        coefficient_kernel,
        "coefficients",
        [place, wind, a_own] + state[1:],
        [((5, NX + 2 * H, 8 * (TILES + 2), NZ), VMEM)],
        [pltpu.VMEM(wide, F32), pltpu.VMEM((NZ, NZ), jnp.bfloat16), DMA((7,))],
        [SMEM, SMEM] + [VMEM] * 7,
        3,
        6,
    )[0]


SHIFT = 8 - H


def sweep(number, src, dst, scaled, coef):
    nx, ny = src.shape[:2]
    last = lax.broadcasted_iota(jnp.int32, (G, 128), 1) == 127
    block = 2

    def row(ref, x, y, z):
        return ref[x, y, :, z * 128 : (z + 1) * 128]

    def rows(ref, x, y):
        return [row(ref, x, y, z) for z in (0, 1)]

    def spread(k, x, y, z):
        y = y + SHIFT
        return jnp.broadcast_to(coef[k, x, y : y + 1, z * 128 : (z + 1) * 128], (G, 128))

    def planes(i, carry):
        xs = [number + block * i + k for k in range(block)]
        below = [rows(src, x, number - 1) for x in xs]
        here = [rows(src, x, number) for x in xs]
        for y in range(number, ny - number):
            above = [rows(src, x, y + 1) for x in xs]
            beside = [rows(src, xs[0] - 1, y)] + here + [rows(src, xs[-1] + 1, y)]
            for k, x in enumerate(xs):
                even, odd = here[k]
                up = [odd, jnp.where(last, 0.0, pltpu.roll(even, 127, 1))]
                down = [pltpu.roll(odd, 1, 1), even]
                for z in (0, 1):
                    if number == 1:
                        part = here[k][z] * spread(4, x, y, z)
                        scaled[x, y, :, z * 128 : (z + 1) * 128] = part
                    else:
                        part = row(scaled, x, y, z)
                    part = part + spread(0, x, y, z) * (beside[k + 2][z] + (above[k][z] + up[z]))
                    other = spread(1, x, y, z) * beside[k][z] + spread(2, x, y, z) * below[k][z]
                    dst[x, y, :, z * 128 : (z + 1) * 128] = (part + spread(3, x, y, z) * down[z]) + other
            below, here = here, above
        return carry

    lax.fori_loop(0, (nx - 2 * number) // block, planes, 0)


def gather_state(place, field, a_in, b_in, c_in, d_in, f_in, h_in, u, sems):
    outer, own_x, own_y, rows = pl.ds(place[8], H), pl.ds(H, NX), pl.ds(H, NY), pl.ds(0, H)
    copy_all(
        [
            (field, u.at[own_x, own_y]),
            (a_in.at[:, pl.ds(0, NY + 2 * H)], u.at[pl.ds(place[9], H)]),
            (b_in.at[:, pl.ds(0, NY)], u.at[outer, own_y]),
            (c_in.at[:, rows], u.at[own_x, pl.ds(place[4], H)]),
            (d_in.at[:, rows], u.at[own_x, pl.ds(place[5], H)]),
            (f_in.at[:, rows], u.at[outer, pl.ds(place[4], H)]),
            (h_in.at[:, rows], u.at[outer, pl.ds(place[5], H)]),
        ],
        sems,
    )


def sweeps(u, v, scaled, coef):
    for number in range(1, SWEEPS + 1):
        sweep(number, u, v, scaled, coef)
        u, v = v, u


def step_kernel(place, *refs):
    state, coef, s_out, outs = refs[:7], refs[7], refs[8], refs[9:14]
    u, v, scaled, sems = refs[14:]
    gather_state(place, *state, u, sems)
    sweeps(u, v, scaled, coef)
    own = u.at[pl.ds(H, NX), pl.ds(H, NY)]
    copy_all(face_pairs(u, place, H, H, outs) + [(own, s_out)], sems)


STATE_SCRATCH = [pltpu.VMEM((NX + 2 * H, NY + 2 * H, G, NZ), F32)] * 3


def step(g, place, state):
    return kernel(
        step_kernel,
        f"step{g}",
        [place, *state],
        [((NX, NY, G, NZ), VMEM)] + face_outs(False),
        STATE_SCRATCH + [DMA((8,))],
        [SMEM] + [VMEM] * 8,
        12,
        24,
    )


def read_sensors(cells, u, out):
    lane = lax.broadcasted_iota(jnp.int32, (G, 128), 1)

    def one(s, found):
        cell = cells[s]
        x, y, z = cell // (NY * NZ), (cell // NZ) % NY, cell % NZ
        half = pl.multiple_of((z % 2) * 128, 128)
        value = pltpu.roll(u[x + H, y + H, :, pl.ds(half, 128)], (s - z // 2 + 128) % 128, 1)
        return jnp.where(lane == s, value, found)

    out[...] = lax.fori_loop(0, 128, one, jnp.zeros((G, 128), F32), unroll=8)


def last_kernel(g, place, cells, *rest):
    state, coef = rest[:7], rest[7]
    out, reading, u, v, scaled, stage, mat, sems, sem_out = rest[-9:]
    gather_state(place, *state, u, sems)
    mat[...] = sorting(True)
    sweeps(u, v, scaled, coef)

    def store(i):
        dst = out.at[pl.ds(g * G, G), pl.ds(i * PLANES, PLANES)]
        return pltpu.make_async_copy(stage.at[:, pl.ds(i * PLANES, PLANES)], dst, sem_out.at[i])

    def planes(i, carry):
        rows = u[pl.ds(i * PLANES + H, PLANES), pl.ds(H, NY)].reshape(PLANES * NY * G, NZ)
        rows = reorder(rows, mat[...]).reshape(PLANES, NY, G, NZ)
        for k in range(PLANES):
            stage[:, i * PLANES + k] = jnp.swapaxes(rows[k], 0, 1)
        store(i).start()
        return carry

    lax.fori_loop(0, NX // PLANES, planes, 0)
    read_sensors(cells, u, reading)
    for i in range(NX // PLANES):
        store(i).wait()


def last_step(g, place, cells, state, fields=None):
    more = [] if fields is None else [fields]
    return kernel(
        functools.partial(last_kernel, g),
        f"last{g}",
        [place, cells, *state] + more,
        [((2 * G, NX, NY, NZ), ANY), ((G, 128), VMEM)],
        STATE_SCRATCH
        + [
            pltpu.VMEM((G, NX, NY, NZ), F32),
            pltpu.VMEM((NZ, NZ), jnp.bfloat16),
            DMA((8,)),
            DMA((NX // PLANES,)),
        ],
        [SMEM, SMEM] + [VMEM] * 8 + [ANY] * len(more),
        16,
        30,
        {10: 0} if more else {},
    )


def readings_exchange(readings, sensor_owner, sensor_count, goal_weight):
    probe_count, sensor_rows = readings.shape
    goal_count = goal_weight.shape[3]
    device_count = lax.axis_size(ALL)
    capacity = max(2, (sensor_rows + device_count - 1) // device_count)
    row_index = jnp.arange(sensor_rows, dtype=jnp.int32)
    active = (row_index < sensor_count.reshape(())).astype(F32)
    readings = readings.T * active[:, None]
    weights = goal_weight.reshape(sensor_rows, goal_count)
    owners = sensor_owner.reshape(sensor_rows)
    earlier = (owners[None, :] == owners[:, None]) & (row_index[None, :] < row_index[:, None])
    slot_rank = jnp.sum(earlier.astype(jnp.int32), axis=1)
    slot_index = owners * capacity + slot_rank
    slots = jnp.arange(device_count * capacity, dtype=jnp.int32)
    placing = (slots[:, None] == slot_index[None, :]).astype(F32)
    payload = jnp.concatenate([readings, weights], axis=1)
    outgoing = jnp.dot(placing, payload, precision=lax.Precision.HIGHEST)
    outgoing = outgoing.reshape(device_count, capacity, probe_count + goal_count)
    received = lax.all_to_all(outgoing, ALL, split_axis=0, concat_axis=0, tiled=True)
    received = received.reshape(device_count * capacity, probe_count + goal_count)
    goal_block = jnp.dot(
        received[:, probe_count:].T, received[:, :probe_count], precision=lax.Precision.HIGHEST
    )
    own = jnp.dot(goal_block.T, goal_block, precision=lax.Precision.HIGHEST)
    terms = jnp.broadcast_to(own.reshape(1, -1), (device_count, own.size))
    terms = lax.all_to_all(terms, ALL, split_axis=0, concat_axis=0, tiled=True)
    return goal_block, jnp.sum(terms, axis=0).reshape(own.shape)


def body(probes, diffusivity, wind_speed, sensor_cell, sensor_owner, sensor_count, goal_weight):
    core = lax.axis_index("gx_2")
    odd = lax.axis_index("gy") % 2

    def either(flag, zero, one):
        return jnp.where(flag == 0, zero, one)

    place = jnp.stack(
        [
            either(core, 0, NX - H),
            either(core, NX - H, 0),
            either(odd, NY - H, 0),
            either(odd, 0, NY - H),
            either(odd, NY + H, 0),
            either(odd, 0, NY + H),
            0,
            0,
            either(core, 0, NX + H),
            either(core, NX + H, 0),
            either(odd, TILES - 1, 0),
            either(odd, 0, TILES - 1),
            either(odd, TILES + 1, 0),
            either(odd, 0, TILES + 1),
        ]
    ).astype(jnp.int32)
    peers_x, peers_y = lax.axis_size(GX), lax.axis_size("gy")
    inner = both([(i, i + 1) for i in range(0, peers_x - 1, 2)])
    outer = both([(i, i + 1) for i in range(1, peers_x - 1, 2)])
    first = both([(i, i + 1) for i in range(0, peers_y - 1, 2)])
    second = both([(i, i + 1) for i in range(1, peers_y - 1, 2)])

    def across(pairs_x, pairs_y):
        return [(i * peers_y + k, j * peers_y + n) for i, j in pairs_x for k, n in pairs_y]

    def exchange(b, c, d, f, h):
        return [
            lax.ppermute(b, GX, outer),
            lax.ppermute(c, "gy", first),
            lax.ppermute(d, "gy", second),
            lax.ppermute(f, ALL, across(outer, first)),
            lax.ppermute(h, ALL, across(outer, second)),
        ]

    def after(*values):
        return list(lax.optimization_barrier(values))

    probes = pltpu.with_memory_space_constraint(probes, pltpu.HBM)
    a_own = diffusivity.reshape(NX, TILES, 8, NZ)
    cells = sensor_cell.reshape(-1)
    made = [pack(0, place, probes, a_own), pack(1, place, probes, a_own)]
    arrived = exchange(*made[0][1:])
    joined = after(*arrived, *made[1])
    arrived, made[1] = joined[:5], joined[5:]
    coef = fields = None
    readings = []
    for turn in range(4):
        g, field = turn % 2, made[turn][0]
        a = inner_planes(place, field, *arrived[1:3], *([a_own] if turn == 0 else []))
        state = [field, lax.ppermute(a, GX, inner), *arrived]
        if turn < 3:
            leaving = after(*made[turn + 1][1:], a)[:5]
            arrived = exchange(*leaving)
        if turn == 0:
            coef = coefficients(place, wind_speed, a_own, state)
        if turn < 2:
            joined = after(*arrived, *step(g, place, state + [coef]))
            arrived = joined[:5]
            made.append(joined[5:])
        else:
            fields, reading = last_step(g, place, cells, state + [coef], fields)
            readings.append(reading)
            if turn == 2:
                *arrived, fields = after(*arrived, fields)
    readings = jnp.concatenate(readings, axis=0)
    goal_block, ritz_gram = readings_exchange(readings, sensor_owner, sensor_count, goal_weight)
    return fields, goal_block, ritz_gram


def solution(mesh):
    torus = Mesh(mesh.devices.reshape(4, 4, 2, mesh.shape["gy"]), ALL)
    return jax.shard_map(
        body,
        mesh=torus,
        in_specs=(
            P(None, GX, "gy", None),
            P(GX, "gy", None),
            P(),
            P(GX, "gy", None),
            P(GX, "gy", None, None),
            P(GX, "gy"),
            P(GX, "gy", None, None),
        ),
        out_specs=(P(None, GX, "gy", None), P(ALL, None), P()),
        check_vma=False,
    )
```

```python
import functools

import jax
import jax.numpy as jnp
from jax import lax
from jax.experimental import pallas as pl
from jax.experimental.pallas import tpu as pltpu
from jax.sharding import Mesh
from jax.sharding import PartitionSpec as P

SWEEPS = 4
H = SWEEPS
ALL = ("gx_0", "gx_1", "gx_2", "gy")
GX = ("gx_0", "gx_1", "gx_2")
G = 8
TAU = 2.0
F32 = jnp.float32
ANY = pl.BlockSpec(memory_space=pl.ANY)
SMEM = pl.BlockSpec(memory_space=pltpu.SMEM)
VMEM = pl.BlockSpec(memory_space=pltpu.VMEM)
DMA = pltpu.SemaphoreType.DMA
NX, NY, NZ = 16, 32, 256
TILES = NY // 8


def both(pairs):
    return pairs + [(b, a) for a, b in pairs]


def near(x):
    return pltpu.with_memory_space_constraint(x, pltpu.VMEM)


def kernel(body, name, operands, outs, scratch, in_specs, microseconds, mib, aliases=None):
    placed = [near(x) if spec is VMEM else x for x, spec in zip(operands, in_specs)]
    out_shape = [pltpu.VMEM(dims, F32) if spec is VMEM else jax.ShapeDtypeStruct(dims, F32) for dims, spec in outs]
    return pl.pallas_call(
        body,
        in_specs=in_specs,
        out_specs=[spec for _, spec in outs],
        out_shape=out_shape,
        scratch_shapes=scratch,
        input_output_aliases=aliases or {},
        compiler_params=pltpu.CompilerParams(vmem_limit_bytes=mib * 1024 * 1024),
        cost_estimate=pl.CostEstimate(flops=0, transcendentals=0, bytes_accessed=int(microseconds * 3.5e6)),
        name=name,
    )(*placed)


def sorting(inverse):
    row = lax.broadcasted_iota(jnp.int32, (NZ, NZ), 0)
    col = lax.broadcasted_iota(jnp.int32, (NZ, NZ), 1)
    if inverse:
        row, col = col, row
    source = jnp.where(col < NZ // 2, 2 * col, 2 * col - (NZ - 1))
    return (row == source).astype(F32).astype(jnp.bfloat16)


def reorder(v, matrix):
    high = v.astype(jnp.bfloat16)
    rest = v - high.astype(F32)
    mid = rest.astype(jnp.bfloat16)
    low = (rest - mid.astype(F32)).astype(jnp.bfloat16)
    dot = functools.partial(jnp.dot, preferred_element_type=F32)
    return dot(high, matrix) + (dot(mid, matrix) + dot(low, matrix))


def start_all(pairs, sems, first=0):
    made = [pltpu.make_async_copy(a, b, sems.at[first + i]) for i, (a, b) in enumerate(pairs)]
    for c in made:
        c.start()
    return made


def copy_all(pairs, sems):
    for c in start_all(pairs, sems):
        c.wait()


def face_pairs(field, place, x0, y0, outs):
    planes, all_x, all_y = pl.ds(x0 + place[0], H), pl.ds(x0, NX), pl.ds(y0, NY)
    c_rows, d_rows = pl.ds(y0 + place[2], H), pl.ds(y0 + place[3], H)
    taken = [(planes, all_y), (all_x, c_rows), (all_x, d_rows), (planes, c_rows), (planes, d_rows)]
    return [(field.at[x, y], out.at[:, pl.ds(0, NY if y is all_y else H)]) for (x, y), out in zip(taken, outs)]


def face_outs(extra):
    more = 1 if extra else 0
    faces = [(H, NY + TILES * more, G, NZ)] + [(NX, H + more, G, NZ)] * 2 + [(H, H + more, G, NZ)] * 2
    return [(dims, VMEM) for dims in faces]


PLANES = 4


def pack_kernel(g, place, probes, *rest):
    a_in = rest[0] if g == 0 else None
    s_out, *outs = rest[-10:-4]
    raw, mat, sem_in, sem_f = rest[-4:]

    def load(i):
        src = probes.at[pl.ds(g * G, G), pl.ds(i * PLANES, PLANES)]
        return pltpu.make_async_copy(src, raw.at[:, pl.ds(i * PLANES, PLANES)], sem_in.at[i])

    for i in range(NX // PLANES):
        load(i).start()
    early = []
    if g == 0:
        planes_out, c_tile, d_tile = pl.ds(place[0], H), pl.ds(place[10], 1), pl.ds(place[11], 1)
        pairs = [
            (a_in.at[planes_out], outs[0].at[:, pl.ds(NY, TILES)]),
            (a_in.at[:, c_tile], outs[1].at[:, pl.ds(H, 1)]),
            (a_in.at[:, d_tile], outs[2].at[:, pl.ds(H, 1)]),
            (a_in.at[planes_out, c_tile], outs[3].at[:, pl.ds(H, 1)]),
            (a_in.at[planes_out, d_tile], outs[4].at[:, pl.ds(H, 1)]),
        ]
        early = start_all(pairs, sem_f, 5)
    mat[...] = sorting(False)

    def planes(i, carry):
        load(i).wait()
        rows = [jnp.swapaxes(raw[:, i * PLANES + k], 0, 1).reshape(NY * G, NZ) for k in range(PLANES)]
        rows = reorder(jnp.concatenate(rows, axis=0), mat[...])
        s_out[pl.ds(i * PLANES, PLANES)] = rows.reshape(PLANES, NY, G, NZ)
        return carry

    lax.fori_loop(0, NX // PLANES, planes, 0)
    copy_all(face_pairs(s_out, place, 0, 0, outs), sem_f)
    for c in early:
        c.wait()


def pack(g, place, probes, a):
    more = [pltpu.with_memory_space_constraint(a, pltpu.HBM)] if g == 0 else []
    return kernel(
        functools.partial(pack_kernel, g),
        f"pack{g}",
        [place, probes] + more,
        [((NX, NY, G, NZ), VMEM)] + face_outs(g == 0),
        [
            pltpu.VMEM((G, NX, NY, NZ), F32),
            pltpu.VMEM((NZ, NZ), jnp.bfloat16),
            DMA((NX // PLANES,)),
            DMA((10,)),
        ],
        [SMEM, ANY] + [ANY] * len(more),
        6,
        12,
    )


def inner_kernel(place, field, c_in, d_in, *rest):
    out, sems = rest[-2:]
    inner, rows = pl.ds(place[1], H), pl.ds(0, H)
    pairs = [
        (field.at[inner], out.at[:, pl.ds(H, NY)]),
        (c_in.at[inner, rows], out.at[:, pl.ds(place[4], H)]),
        (d_in.at[inner, rows], out.at[:, pl.ds(place[5], H)]),
    ]
    if len(rest) > 2:
        tile, base = pl.ds(H, 1), NY + 2 * H
        pairs += [
            (rest[0].at[inner], out.at[:, pl.ds(base + 1, TILES)]),
            (c_in.at[inner, tile], out.at[:, pl.ds(base + place[12], 1)]),
            (d_in.at[inner, tile], out.at[:, pl.ds(base + place[13], 1)]),
        ]
    copy_all(pairs, sems)


def inner_planes(place, field, c_in, d_in, a=None):
    more = [] if a is None else [a]
    n = len(more)
    return kernel(
        inner_kernel,
        "inner",
        [place, field, c_in, d_in] + more,
        [((H, NY + 2 * H + (TILES + 2) * n, G, NZ), VMEM)],
        [DMA((6,))],
        [SMEM] + [VMEM] * (3 + n),
        1,
        2,
    )[0]


def coefficient_kernel(place, wind, a_own, a_in, b_in, c_in, d_in, f_in, h_in, out, wide, mat, sems):
    base = NY + 2 * H
    outer, own, tile = pl.ds(place[8], H), pl.ds(1, TILES), pl.ds(H, 1)
    copy_all(
        [
            (a_own, wide.at[pl.ds(H, NX), own]),
            (a_in.at[:, pl.ds(base, TILES + 2)], wide.at[pl.ds(place[9], H)]),
            (b_in.at[:, pl.ds(NY, TILES)], wide.at[outer, own]),
            (c_in.at[:, tile], wide.at[pl.ds(H, NX), pl.ds(place[12], 1)]),
            (d_in.at[:, tile], wide.at[pl.ds(H, NX), pl.ds(place[13], 1)]),
            (f_in.at[:, tile], wide.at[outer, pl.ds(place[12], 1)]),
            (h_in.at[:, tile], wide.at[outer, pl.ds(place[13], 1)]),
        ],
        sems,
    )
    mat[...] = sorting(False)
    w = [wind[i] for i in range(3)]
    count = 8 * (TILES + 2)

    def planes(i, carry):
        x = pl.ds(i * H, H)
        a = reorder(wide[x].reshape(H * count, NZ), mat[...])
        inverse = 1.0 / (1.0 + TAU * (6.0 * a + (w[0] + w[1] + w[2])))
        inverse = jnp.where(a > 0.0, inverse, 0.0)
        spread = TAU * a * inverse
        lane = lax.broadcasted_iota(jnp.int32, a.shape, 1)
        parts = [
            spread,
            spread + (TAU * w[0]) * inverse,
            spread + (TAU * w[1]) * inverse,
            jnp.where(lane == 0, 0.0, spread + (TAU * w[2]) * inverse),
            inverse,
        ]
        for k, part in enumerate(parts):
            out[k, x] = part.reshape(H, count, NZ)
        return carry

    lax.fori_loop(0, (NX + 2 * H) // H, planes, 0)


def coefficients(place, wind, a_own, state):
    wide = (NX + 2 * H, TILES + 2, 8, NZ)
    return kernel(
        coefficient_kernel,
        "coefficients",
        [place, wind, a_own] + state[1:],
        [((5, NX + 2 * H, 8 * (TILES + 2), NZ), VMEM)],
        [pltpu.VMEM(wide, F32), pltpu.VMEM((NZ, NZ), jnp.bfloat16), DMA((7,))],
        [SMEM, SMEM] + [VMEM] * 7,
        3,
        6,
    )[0]


SHIFT = 8 - H


def sweep(number, src, dst, scaled, coef):
    nx, ny = src.shape[:2]
    last = lax.broadcasted_iota(jnp.int32, (G, 128), 1) == 127
    block = 2 if (nx - 2 * number) % 4 else 4

    def row(ref, x, y, z):
        return ref[x, y, :, z * 128 : (z + 1) * 128]

    def rows(ref, x, y):
        return [row(ref, x, y, z) for z in (0, 1)]

    def spread(k, x, y, z):
        y = y + SHIFT
        return jnp.broadcast_to(coef[k, x, y : y + 1, z * 128 : (z + 1) * 128], (G, 128))

    def planes(i, carry):
        xs = [number + block * i + k for k in range(block)]
        below = [rows(src, x, number - 1) for x in xs]
        here = [rows(src, x, number) for x in xs]
        for y in range(number, ny - number):
            above = [rows(src, x, y + 1) for x in xs]
            beside = [rows(src, xs[0] - 1, y)] + here + [rows(src, xs[-1] + 1, y)]
            for k, x in enumerate(xs):
                even, odd = here[k]
                up = [odd, jnp.where(last, 0.0, pltpu.roll(even, 127, 1))]
                down = [pltpu.roll(odd, 1, 1), even]
                for z in (0, 1):
                    if number == 1:
                        part = here[k][z] * spread(4, x, y, z)
                        scaled[x, y, :, z * 128 : (z + 1) * 128] = part
                    else:
                        part = row(scaled, x, y, z)
                    part = part + spread(0, x, y, z) * (beside[k + 2][z] + (above[k][z] + up[z]))
                    other = spread(1, x, y, z) * beside[k][z] + spread(2, x, y, z) * below[k][z]
                    dst[x, y, :, z * 128 : (z + 1) * 128] = (part + spread(3, x, y, z) * down[z]) + other
            below, here = here, above
        return carry

    lax.fori_loop(0, (nx - 2 * number) // block, planes, 0)


def gather_state(place, field, a_in, b_in, c_in, d_in, f_in, h_in, u, sems):
    outer, own_x, own_y, rows = pl.ds(place[8], H), pl.ds(H, NX), pl.ds(H, NY), pl.ds(0, H)
    copy_all(
        [
            (field, u.at[own_x, own_y]),
            (a_in.at[:, pl.ds(0, NY + 2 * H)], u.at[pl.ds(place[9], H)]),
            (b_in.at[:, pl.ds(0, NY)], u.at[outer, own_y]),
            (c_in.at[:, rows], u.at[own_x, pl.ds(place[4], H)]),
            (d_in.at[:, rows], u.at[own_x, pl.ds(place[5], H)]),
            (f_in.at[:, rows], u.at[outer, pl.ds(place[4], H)]),
            (h_in.at[:, rows], u.at[outer, pl.ds(place[5], H)]),
        ],
        sems,
    )


def sweeps(u, v, scaled, coef):
    for number in range(1, SWEEPS + 1):
        sweep(number, u, v, scaled, coef)
        u, v = v, u


def step_kernel(place, *refs):
    state, coef, s_out, outs = refs[:7], refs[7], refs[8], refs[9:14]
    u, v, scaled, sems = refs[14:]
    gather_state(place, *state, u, sems)
    sweeps(u, v, scaled, coef)
    own = u.at[pl.ds(H, NX), pl.ds(H, NY)]
    copy_all(face_pairs(u, place, H, H, outs) + [(own, s_out)], sems)


STATE_SCRATCH = [pltpu.VMEM((NX + 2 * H, NY + 2 * H, G, NZ), F32)] * 3


def step(g, place, state):
    return kernel(
        step_kernel,
        f"step{g}",
        [place, *state],
        [((NX, NY, G, NZ), VMEM)] + face_outs(False),
        STATE_SCRATCH + [DMA((8,))],
        [SMEM] + [VMEM] * 8,
        12,
        24,
    )


def read_sensors(cells, u, out):
    lane = lax.broadcasted_iota(jnp.int32, (G, 128), 1)

    def one(s, found):
        cell = cells[s]
        x, y, z = cell // (NY * NZ), (cell // NZ) % NY, cell % NZ
        half = pl.multiple_of((z % 2) * 128, 128)
        value = pltpu.roll(u[x + H, y + H, :, pl.ds(half, 128)], (s - z // 2 + 128) % 128, 1)
        return jnp.where(lane == s, value, found)

    out[...] = lax.fori_loop(0, 128, one, jnp.zeros((G, 128), F32), unroll=8)


def last_kernel(g, place, cells, *rest):
    state, coef = rest[:7], rest[7]
    out, reading, u, v, scaled, stage, mat, sems, sem_out = rest[-9:]
    gather_state(place, *state, u, sems)
    mat[...] = sorting(True)
    sweeps(u, v, scaled, coef)

    def store(i):
        dst = out.at[pl.ds(g * G, G), pl.ds(i * PLANES, PLANES)]
        return pltpu.make_async_copy(stage.at[:, pl.ds(i * PLANES, PLANES)], dst, sem_out.at[i])

    def planes(i, carry):
        rows = u[pl.ds(i * PLANES + H, PLANES), pl.ds(H, NY)].reshape(PLANES * NY * G, NZ)
        rows = reorder(rows, mat[...]).reshape(PLANES, NY, G, NZ)
        for k in range(PLANES):
            stage[:, i * PLANES + k] = jnp.swapaxes(rows[k], 0, 1)
        store(i).start()
        return carry

    lax.fori_loop(0, NX // PLANES, planes, 0)
    read_sensors(cells, u, reading)
    for i in range(NX // PLANES):
        store(i).wait()


def last_step(g, place, cells, state, fields=None):
    more = [] if fields is None else [fields]
    return kernel(
        functools.partial(last_kernel, g),
        f"last{g}",
        [place, cells, *state] + more,
        [((2 * G, NX, NY, NZ), ANY), ((G, 128), VMEM)],
        STATE_SCRATCH
        + [
            pltpu.VMEM((G, NX, NY, NZ), F32),
            pltpu.VMEM((NZ, NZ), jnp.bfloat16),
            DMA((8,)),
            DMA((NX // PLANES,)),
        ],
        [SMEM, SMEM] + [VMEM] * 8 + [ANY] * len(more),
        16,
        30,
        {10: 0} if more else {},
    )


def readings_exchange(readings, sensor_owner, sensor_count, goal_weight):
    probe_count, sensor_rows = readings.shape
    goal_count = goal_weight.shape[3]
    device_count = lax.axis_size(ALL)
    capacity = max(2, (sensor_rows + device_count - 1) // device_count)
    row_index = jnp.arange(sensor_rows, dtype=jnp.int32)
    active = (row_index < sensor_count.reshape(())).astype(F32)
    readings = readings.T * active[:, None]
    weights = goal_weight.reshape(sensor_rows, goal_count)
    owners = sensor_owner.reshape(sensor_rows)
    earlier = (owners[None, :] == owners[:, None]) & (row_index[None, :] < row_index[:, None])
    slot_rank = jnp.sum(earlier.astype(jnp.int32), axis=1)
    slot_index = owners * capacity + slot_rank
    slots = jnp.arange(device_count * capacity, dtype=jnp.int32)
    placing = (slots[:, None] == slot_index[None, :]).astype(F32)
    payload = jnp.concatenate([readings, weights], axis=1)
    outgoing = jnp.dot(placing, payload, precision=lax.Precision.HIGHEST)
    outgoing = outgoing.reshape(device_count, capacity, probe_count + goal_count)
    received = lax.all_to_all(outgoing, ALL, split_axis=0, concat_axis=0, tiled=True)
    received = received.reshape(device_count * capacity, probe_count + goal_count)
    goal_block = jnp.dot(
        received[:, probe_count:].T, received[:, :probe_count], precision=lax.Precision.HIGHEST
    )
    own = jnp.dot(goal_block.T, goal_block, precision=lax.Precision.HIGHEST)
    terms = jnp.broadcast_to(own.reshape(1, -1), (device_count, own.size))
    terms = lax.all_to_all(terms, ALL, split_axis=0, concat_axis=0, tiled=True)
    return goal_block, jnp.sum(terms, axis=0).reshape(own.shape)


def body(probes, diffusivity, wind_speed, sensor_cell, sensor_owner, sensor_count, goal_weight):
    core = lax.axis_index("gx_2")
    odd = lax.axis_index("gy") % 2

    def either(flag, zero, one):
        return jnp.where(flag == 0, zero, one)

    place = jnp.stack(
        [
            either(core, 0, NX - H),
            either(core, NX - H, 0),
            either(odd, NY - H, 0),
            either(odd, 0, NY - H),
            either(odd, NY + H, 0),
            either(odd, 0, NY + H),
            0,
            0,
            either(core, 0, NX + H),
            either(core, NX + H, 0),
            either(odd, TILES - 1, 0),
            either(odd, 0, TILES - 1),
            either(odd, TILES + 1, 0),
            either(odd, 0, TILES + 1),
        ]
    ).astype(jnp.int32)
    peers_x, peers_y = lax.axis_size(GX), lax.axis_size("gy")
    inner = both([(i, i + 1) for i in range(0, peers_x - 1, 2)])
    outer = both([(i, i + 1) for i in range(1, peers_x - 1, 2)])
    first = both([(i, i + 1) for i in range(0, peers_y - 1, 2)])
    second = both([(i, i + 1) for i in range(1, peers_y - 1, 2)])

    def across(pairs_x, pairs_y):
        return [(i * peers_y + k, j * peers_y + n) for i, j in pairs_x for k, n in pairs_y]

    def exchange(b, c, d, f, h):
        return [
            lax.ppermute(b, GX, outer),
            lax.ppermute(c, "gy", first),
            lax.ppermute(d, "gy", second),
            lax.ppermute(f, ALL, across(outer, first)),
            lax.ppermute(h, ALL, across(outer, second)),
        ]

    def after(*values):
        return list(lax.optimization_barrier(values))

    probes = pltpu.with_memory_space_constraint(probes, pltpu.HBM)
    a_own = diffusivity.reshape(NX, TILES, 8, NZ)
    cells = sensor_cell.reshape(-1)
    made = [pack(0, place, probes, a_own), pack(1, place, probes, a_own)]
    arrived = exchange(*made[0][1:])
    queued = exchange(*made[1][1:4], *after(*made[1][4:], *arrived[3:])[:2])
    joined = after(*arrived, *made[1], *queued[3:])
    arrived, made[1], queued[3:] = joined[:5], joined[5:11], joined[11:]
    coef = fields = None
    readings = []
    for turn in range(4):
        g, field = turn % 2, made[turn][0]
        a = inner_planes(place, field, *arrived[1:3], *([a_own] if turn == 0 else []))
        state = [field, lax.ppermute(a, GX, inner), *arrived]
        if turn == 0:
            arrived = queued
        elif turn < 3:
            leaving = after(*made[turn + 1][1:], a)[:5]
            arrived = exchange(*leaving)
        if turn == 0:
            coef = coefficients(place, wind_speed, a_own, state)
        if turn < 2:
            joined = after(*arrived, *step(g, place, state + [coef]))
            arrived = joined[:5]
            made.append(joined[5:])
        else:
            fields, reading = last_step(g, place, cells, state + [coef], fields)
            readings.append(reading)
            if turn == 2:
                *arrived, fields = after(*arrived, fields)
    readings = jnp.concatenate(readings, axis=0)
    goal_block, ritz_gram = readings_exchange(readings, sensor_owner, sensor_count, goal_weight)
    return fields, goal_block, ritz_gram


def solution(mesh):
    torus = Mesh(mesh.devices.reshape(4, 4, 2, mesh.shape["gy"]), ALL)
    return jax.shard_map(
        body,
        mesh=torus,
        in_specs=(
            P(None, GX, "gy", None),
            P(GX, "gy", None),
            P(),
            P(GX, "gy", None),
            P(GX, "gy", None, None),
            P(GX, "gy"),
            P(GX, "gy", None, None),
        ),
        out_specs=(P(None, GX, "gy", None), P(ALL, None), P()),
        check_vma=False,
    )
```

```python
import functools

import jax
import jax.numpy as jnp
from jax import lax
from jax.experimental import pallas as pl
from jax.experimental.pallas import tpu as pltpu
from jax.sharding import Mesh
from jax.sharding import PartitionSpec as P

SWEEPS = 4
H = SWEEPS
ALL = ("gx_0", "gx_1", "gx_2", "gy")
GX = ("gx_0", "gx_1", "gx_2")
G = 8
TAU = 2.0
F32 = jnp.float32
ANY = pl.BlockSpec(memory_space=pl.ANY)
SMEM = pl.BlockSpec(memory_space=pltpu.SMEM)
VMEM = pl.BlockSpec(memory_space=pltpu.VMEM)
DMA = pltpu.SemaphoreType.DMA
NX, NY, NZ = 16, 32, 256
TILES = NY // 8


def both(pairs):
    return pairs + [(b, a) for a, b in pairs]


def near(x):
    return pltpu.with_memory_space_constraint(x, pltpu.VMEM)


def kernel(body, name, operands, outs, scratch, in_specs, microseconds, mib, aliases=None):
    placed = [near(x) if spec is VMEM else x for x, spec in zip(operands, in_specs)]
    out_shape = [pltpu.VMEM(dims, F32) if spec is VMEM else jax.ShapeDtypeStruct(dims, F32) for dims, spec in outs]
    return pl.pallas_call(
        body,
        in_specs=in_specs,
        out_specs=[spec for _, spec in outs],
        out_shape=out_shape,
        scratch_shapes=scratch,
        input_output_aliases=aliases or {},
        compiler_params=pltpu.CompilerParams(vmem_limit_bytes=mib * 1024 * 1024),
        cost_estimate=pl.CostEstimate(flops=0, transcendentals=0, bytes_accessed=int(microseconds * 3.5e6)),
        name=name,
    )(*placed)


def sorting(inverse):
    row = lax.broadcasted_iota(jnp.int32, (NZ, NZ), 0)
    col = lax.broadcasted_iota(jnp.int32, (NZ, NZ), 1)
    if inverse:
        row, col = col, row
    source = jnp.where(col < NZ // 2, 2 * col, 2 * col - (NZ - 1))
    return (row == source).astype(F32).astype(jnp.bfloat16)


def reorder(v, matrix):
    high = v.astype(jnp.bfloat16)
    rest = v - high.astype(F32)
    mid = rest.astype(jnp.bfloat16)
    low = (rest - mid.astype(F32)).astype(jnp.bfloat16)
    dot = functools.partial(jnp.dot, preferred_element_type=F32)
    return dot(high, matrix) + (dot(mid, matrix) + dot(low, matrix))


def start_all(pairs, sems, first=0):
    made = [pltpu.make_async_copy(a, b, sems.at[first + i]) for i, (a, b) in enumerate(pairs)]
    for c in made:
        c.start()
    return made


def copy_all(pairs, sems):
    for c in start_all(pairs, sems):
        c.wait()


def face_pairs(field, place, x0, y0, outs):
    planes, all_x, all_y = pl.ds(x0 + place[0], H), pl.ds(x0, NX), pl.ds(y0, NY)
    c_rows, d_rows = pl.ds(y0 + place[2], H), pl.ds(y0 + place[3], H)
    taken = [(planes, all_y), (all_x, c_rows), (all_x, d_rows), (planes, c_rows), (planes, d_rows)]
    return [(field.at[x, y], out.at[:, pl.ds(0, NY if y is all_y else H)]) for (x, y), out in zip(taken, outs)]


def face_outs(extra):
    more = 1 if extra else 0
    faces = [(H, NY + TILES * more, G, NZ)] + [(NX, H + more, G, NZ)] * 2 + [(H, H + more, G, NZ)] * 2
    return [(dims, VMEM) for dims in faces]


PLANES = 4


def pack_kernel(g, place, probes, *rest):
    a_in = rest[0] if g == 0 else None
    s_out, *outs = rest[-10:-4]
    raw, mat, sem_in, sem_f = rest[-4:]

    def load(i):
        src = probes.at[pl.ds(g * G, G), pl.ds(i * PLANES, PLANES)]
        return pltpu.make_async_copy(src, raw.at[:, pl.ds(i * PLANES, PLANES)], sem_in.at[i])

    for i in range(NX // PLANES):
        load(i).start()
    early = []
    if g == 0:
        planes_out, c_tile, d_tile = pl.ds(place[0], H), pl.ds(place[10], 1), pl.ds(place[11], 1)
        pairs = [
            (a_in.at[planes_out], outs[0].at[:, pl.ds(NY, TILES)]),
            (a_in.at[:, c_tile], outs[1].at[:, pl.ds(H, 1)]),
            (a_in.at[:, d_tile], outs[2].at[:, pl.ds(H, 1)]),
            (a_in.at[planes_out, c_tile], outs[3].at[:, pl.ds(H, 1)]),
            (a_in.at[planes_out, d_tile], outs[4].at[:, pl.ds(H, 1)]),
        ]
        early = start_all(pairs, sem_f, 5)
    mat[...] = sorting(False)

    def planes(i, carry):
        load(i).wait()
        rows = [jnp.swapaxes(raw[:, i * PLANES + k], 0, 1).reshape(NY * G, NZ) for k in range(PLANES)]
        rows = reorder(jnp.concatenate(rows, axis=0), mat[...])
        s_out[pl.ds(i * PLANES, PLANES)] = rows.reshape(PLANES, NY, G, NZ)
        return carry

    lax.fori_loop(0, NX // PLANES, planes, 0)
    copy_all(face_pairs(s_out, place, 0, 0, outs), sem_f)
    for c in early:
        c.wait()


def pack(g, place, probes, a):
    more = [pltpu.with_memory_space_constraint(a, pltpu.HBM)] if g == 0 else []
    return kernel(
        functools.partial(pack_kernel, g),
        f"pack{g}",
        [place, probes] + more,
        [((NX, NY, G, NZ), VMEM)] + face_outs(g == 0),
        [
            pltpu.VMEM((G, NX, NY, NZ), F32),
            pltpu.VMEM((NZ, NZ), jnp.bfloat16),
            DMA((NX // PLANES,)),
            DMA((10,)),
        ],
        [SMEM, ANY] + [ANY] * len(more),
        6,
        12,
    )


def inner_kernel(place, field, c_in, d_in, *rest):
    out, sems = rest[-2:]
    inner, rows = pl.ds(place[1], H), pl.ds(0, H)
    pairs = [
        (field.at[inner], out.at[:, pl.ds(H, NY)]),
        (c_in.at[inner, rows], out.at[:, pl.ds(place[4], H)]),
        (d_in.at[inner, rows], out.at[:, pl.ds(place[5], H)]),
    ]
    if len(rest) > 2:
        tile, base = pl.ds(H, 1), NY + 2 * H
        pairs += [
            (rest[0].at[inner], out.at[:, pl.ds(base + 1, TILES)]),
            (c_in.at[inner, tile], out.at[:, pl.ds(base + place[12], 1)]),
            (d_in.at[inner, tile], out.at[:, pl.ds(base + place[13], 1)]),
        ]
    copy_all(pairs, sems)


def inner_planes(place, field, c_in, d_in, a=None):
    more = [] if a is None else [a]
    n = len(more)
    return kernel(
        inner_kernel,
        "inner",
        [place, field, c_in, d_in] + more,
        [((H, NY + 2 * H + (TILES + 2) * n, G, NZ), VMEM)],
        [DMA((6,))],
        [SMEM] + [VMEM] * (3 + n),
        1,
        2,
    )[0]


def coefficient_kernel(place, wind, a_own, a_in, b_in, c_in, d_in, f_in, h_in, out, wide, mat, sems):
    base = NY + 2 * H
    outer, own, tile = pl.ds(place[8], H), pl.ds(1, TILES), pl.ds(H, 1)
    copy_all(
        [
            (a_own, wide.at[pl.ds(H, NX), own]),
            (a_in.at[:, pl.ds(base, TILES + 2)], wide.at[pl.ds(place[9], H)]),
            (b_in.at[:, pl.ds(NY, TILES)], wide.at[outer, own]),
            (c_in.at[:, tile], wide.at[pl.ds(H, NX), pl.ds(place[12], 1)]),
            (d_in.at[:, tile], wide.at[pl.ds(H, NX), pl.ds(place[13], 1)]),
            (f_in.at[:, tile], wide.at[outer, pl.ds(place[12], 1)]),
            (h_in.at[:, tile], wide.at[outer, pl.ds(place[13], 1)]),
        ],
        sems,
    )
    mat[...] = sorting(False)
    w = [wind[i] for i in range(3)]
    count = 8 * (TILES + 2)

    def planes(i, carry):
        x = pl.ds(i * H, H)
        a = reorder(wide[x].reshape(H * count, NZ), mat[...])
        inverse = 1.0 / (1.0 + TAU * (6.0 * a + (w[0] + w[1] + w[2])))
        inverse = jnp.where(a > 0.0, inverse, 0.0)
        spread = TAU * a * inverse
        lane = lax.broadcasted_iota(jnp.int32, a.shape, 1)
        parts = [
            spread,
            spread + (TAU * w[0]) * inverse,
            spread + (TAU * w[1]) * inverse,
            jnp.where(lane == 0, 0.0, spread + (TAU * w[2]) * inverse),
            inverse,
        ]
        for k, part in enumerate(parts):
            out[k, x] = part.reshape(H, count, NZ)
        return carry

    lax.fori_loop(0, (NX + 2 * H) // H, planes, 0)


def coefficients(place, wind, a_own, state):
    wide = (NX + 2 * H, TILES + 2, 8, NZ)
    return kernel(
        coefficient_kernel,
        "coefficients",
        [place, wind, a_own] + state[1:],
        [((5, NX + 2 * H, 8 * (TILES + 2), NZ), VMEM)],
        [pltpu.VMEM(wide, F32), pltpu.VMEM((NZ, NZ), jnp.bfloat16), DMA((7,))],
        [SMEM, SMEM] + [VMEM] * 7,
        3,
        6,
    )[0]


SHIFT = 8 - H


def sweep(number, src, dst, scaled, coef):
    nx, ny = src.shape[:2]
    last = lax.broadcasted_iota(jnp.int32, (G, 128), 1) == 127
    block = 2 if (nx - 2 * number) % 4 else 4

    def row(ref, x, y, z):
        return ref[x, y, :, z * 128 : (z + 1) * 128]

    def rows(ref, x, y):
        return [row(ref, x, y, z) for z in (0, 1)]

    def spread(k, x, y, z):
        y = y + SHIFT
        return jnp.broadcast_to(coef[k, x, y : y + 1, z * 128 : (z + 1) * 128], (G, 128))

    def planes(i, carry):
        xs = [number + block * i + k for k in range(block)]
        below = [rows(src, x, number - 1) for x in xs]
        here = [rows(src, x, number) for x in xs]
        for y in range(number, ny - number):
            above = [rows(src, x, y + 1) for x in xs]
            beside = [rows(src, xs[0] - 1, y)] + here + [rows(src, xs[-1] + 1, y)]
            for k, x in enumerate(xs):
                even, odd = here[k]
                up = [odd, jnp.where(last, 0.0, pltpu.roll(even, 127, 1))]
                down = [pltpu.roll(odd, 1, 1), even]
                for z in (0, 1):
                    if number == 1:
                        part = here[k][z] * spread(4, x, y, z)
                        scaled[x, y, :, z * 128 : (z + 1) * 128] = part
                    else:
                        part = row(scaled, x, y, z)
                    part = part + spread(0, x, y, z) * (beside[k + 2][z] + (above[k][z] + up[z]))
                    other = spread(1, x, y, z) * beside[k][z] + spread(2, x, y, z) * below[k][z]
                    dst[x, y, :, z * 128 : (z + 1) * 128] = (part + spread(3, x, y, z) * down[z]) + other
            below, here = here, above
        return carry

    lax.fori_loop(0, (nx - 2 * number) // block, planes, 0)


def gather_state(place, field, a_in, b_in, c_in, d_in, f_in, h_in, u, sems):
    outer, own_x, own_y, rows = pl.ds(place[8], H), pl.ds(H, NX), pl.ds(H, NY), pl.ds(0, H)
    copy_all(
        [
            (field, u.at[own_x, own_y]),
            (a_in.at[:, pl.ds(0, NY + 2 * H)], u.at[pl.ds(place[9], H)]),
            (b_in.at[:, pl.ds(0, NY)], u.at[outer, own_y]),
            (c_in.at[:, rows], u.at[own_x, pl.ds(place[4], H)]),
            (d_in.at[:, rows], u.at[own_x, pl.ds(place[5], H)]),
            (f_in.at[:, rows], u.at[outer, pl.ds(place[4], H)]),
            (h_in.at[:, rows], u.at[outer, pl.ds(place[5], H)]),
        ],
        sems,
    )


def sweeps(u, v, scaled, coef):
    for number in range(1, SWEEPS + 1):
        sweep(number, u, v, scaled, coef)
        u, v = v, u


def step_kernel(place, *refs):
    state, coef, s_out, outs = refs[:7], refs[7], refs[8], refs[9:14]
    u, v, scaled, sems = refs[14:]
    gather_state(place, *state, u, sems)
    sweeps(u, v, scaled, coef)
    own = u.at[pl.ds(H, NX), pl.ds(H, NY)]
    copy_all(face_pairs(u, place, H, H, outs) + [(own, s_out)], sems)


STATE_SCRATCH = [pltpu.VMEM((NX + 2 * H, NY + 2 * H, G, NZ), F32)] * 3


def step(g, place, state):
    return kernel(
        step_kernel,
        f"step{g}",
        [place, *state],
        [((NX, NY, G, NZ), VMEM)] + face_outs(False),
        STATE_SCRATCH + [DMA((8,))],
        [SMEM] + [VMEM] * 8,
        12,
        24,
    )


def read_sensors(cells, u, out):
    lane = lax.broadcasted_iota(jnp.int32, (G, 128), 1)

    def one(s, found):
        cell = cells[s]
        x, y, z = cell // (NY * NZ), (cell // NZ) % NY, cell % NZ
        half = pl.multiple_of((z % 2) * 128, 128)
        value = pltpu.roll(u[x + H, y + H, :, pl.ds(half, 128)], (s - z // 2 + 128) % 128, 1)
        return jnp.where(lane == s, value, found)

    out[...] = lax.fori_loop(0, 128, one, jnp.zeros((G, 128), F32), unroll=8)


def last_kernel(g, place, cells, *rest):
    state, coef = rest[:7], rest[7]
    out, reading, u, v, scaled, stage, mat, sems, sem_out = rest[-9:]
    gather_state(place, *state, u, sems)
    mat[...] = sorting(True)
    sweeps(u, v, scaled, coef)

    def store(i):
        dst = out.at[pl.ds(g * G, G), pl.ds(i * PLANES, PLANES)]
        return pltpu.make_async_copy(stage.at[:, pl.ds(i * PLANES, PLANES)], dst, sem_out.at[i])

    def planes(i, carry):
        rows = u[pl.ds(i * PLANES + H, PLANES), pl.ds(H, NY)].reshape(PLANES * NY * G, NZ)
        rows = reorder(rows, mat[...]).reshape(PLANES, NY, G, NZ)
        for k in range(PLANES):
            stage[:, i * PLANES + k] = jnp.swapaxes(rows[k], 0, 1)
        store(i).start()
        return carry

    lax.fori_loop(0, NX // PLANES, planes, 0)
    read_sensors(cells, u, reading)
    for i in range(NX // PLANES):
        store(i).wait()


def last_step(g, place, cells, state, fields=None):
    more = [] if fields is None else [fields]
    return kernel(
        functools.partial(last_kernel, g),
        f"last{g}",
        [place, cells, *state] + more,
        [((2 * G, NX, NY, NZ), ANY), ((G, 128), VMEM)],
        STATE_SCRATCH
        + [
            pltpu.VMEM((G, NX, NY, NZ), F32),
            pltpu.VMEM((NZ, NZ), jnp.bfloat16),
            DMA((8,)),
            DMA((NX // PLANES,)),
        ],
        [SMEM, SMEM] + [VMEM] * 8 + [ANY] * len(more),
        16,
        30,
        {10: 0} if more else {},
    )


def readings_exchange(readings, sensor_owner, sensor_count, goal_weight):
    probe_count, sensor_rows = readings.shape
    goal_count = goal_weight.shape[3]
    device_count = lax.axis_size(ALL)
    capacity = max(2, (sensor_rows + device_count - 1) // device_count)
    row_index = jnp.arange(sensor_rows, dtype=jnp.int32)
    active = (row_index < sensor_count.reshape(())).astype(F32)
    readings = readings.T * active[:, None]
    weights = goal_weight.reshape(sensor_rows, goal_count)
    owners = sensor_owner.reshape(sensor_rows)
    earlier = (owners[None, :] == owners[:, None]) & (row_index[None, :] < row_index[:, None])
    slot_rank = jnp.sum(earlier.astype(jnp.int32), axis=1)
    slot_index = owners * capacity + slot_rank
    slots = jnp.arange(device_count * capacity, dtype=jnp.int32)
    placing = (slots[:, None] == slot_index[None, :]).astype(F32)
    payload = jnp.concatenate([readings, weights], axis=1)
    outgoing = jnp.dot(placing, payload, precision=lax.Precision.HIGHEST)
    outgoing = outgoing.reshape(device_count, capacity, probe_count + goal_count)
    received = lax.all_to_all(outgoing, ALL, split_axis=0, concat_axis=0, tiled=True)
    received = received.reshape(device_count * capacity, probe_count + goal_count)
    goal_block = jnp.dot(
        received[:, probe_count:].T, received[:, :probe_count], precision=lax.Precision.HIGHEST
    )
    own = jnp.dot(goal_block.T, goal_block, precision=lax.Precision.HIGHEST)
    terms = jnp.broadcast_to(own.reshape(1, -1), (device_count, own.size))
    terms = lax.all_to_all(terms, ALL, split_axis=0, concat_axis=0, tiled=True)
    return goal_block, jnp.sum(terms, axis=0).reshape(own.shape)


def body(probes, diffusivity, wind_speed, sensor_cell, sensor_owner, sensor_count, goal_weight):
    core = lax.axis_index("gx_2")
    odd = lax.axis_index("gy") % 2

    def either(flag, zero, one):
        return jnp.where(flag == 0, zero, one)

    place = jnp.stack(
        [
            either(core, 0, NX - H),
            either(core, NX - H, 0),
            either(odd, NY - H, 0),
            either(odd, 0, NY - H),
            either(odd, NY + H, 0),
            either(odd, 0, NY + H),
            0,
            0,
            either(core, 0, NX + H),
            either(core, NX + H, 0),
            either(odd, TILES - 1, 0),
            either(odd, 0, TILES - 1),
            either(odd, TILES + 1, 0),
            either(odd, 0, TILES + 1),
        ]
    ).astype(jnp.int32)
    peers_x, peers_y = lax.axis_size(GX), lax.axis_size("gy")
    inner = both([(i, i + 1) for i in range(0, peers_x - 1, 2)])
    outer = both([(i, i + 1) for i in range(1, peers_x - 1, 2)])
    first = both([(i, i + 1) for i in range(0, peers_y - 1, 2)])
    second = both([(i, i + 1) for i in range(1, peers_y - 1, 2)])

    def across(pairs_x, pairs_y):
        return [(i * peers_y + k, j * peers_y + n) for i, j in pairs_x for k, n in pairs_y]

    def sides(b, c, d):
        return [lax.ppermute(b, GX, outer), lax.ppermute(c, "gy", first), lax.ppermute(d, "gy", second)]

    def diagonals(f, h):
        return [lax.ppermute(f, ALL, across(outer, first)), lax.ppermute(h, ALL, across(outer, second))]

    def exchange(b, c, d, f, h):
        return sides(b, c, d) + diagonals(f, h)

    def after(*values):
        return list(lax.optimization_barrier(values))

    probes = pltpu.with_memory_space_constraint(probes, pltpu.HBM)
    a_own = diffusivity.reshape(NX, TILES, 8, NZ)
    cells = sensor_cell.reshape(-1)
    made = [pack(0, place, probes, a_own), pack(1, place, probes, a_own)]
    corner_pairs = zip(made[0][4:], made[1][4:])
    cornered = diagonals(*[jnp.concatenate(pair, axis=1) for pair in corner_pairs])
    arrived = sides(*made[0][1:4]) + cornered
    joined = after(*arrived, *made[1])
    arrived, made[1] = joined[:5], joined[5:]
    coef = fields = None
    readings = []
    for turn in range(4):
        g, field = turn % 2, made[turn][0]
        a = inner_planes(place, field, *arrived[1:3], *([a_own] if turn == 0 else []))
        state = [field, lax.ppermute(a, GX, inner), *arrived]
        if turn == 0:
            arrived = sides(*after(*made[1][1:4], a)[:3]) + [x[:, H + 1 :] for x in arrived[3:]]
        elif turn < 3:
            leaving = after(*made[turn + 1][1:], a)[:5]
            arrived = exchange(*leaving)
        if turn == 0:
            coef = coefficients(place, wind_speed, a_own, state)
        if turn < 2:
            joined = after(*arrived, *step(g, place, state + [coef]))
            arrived = joined[:5]
            made.append(joined[5:])
        else:
            fields, reading = last_step(g, place, cells, state + [coef], fields)
            readings.append(reading)
            if turn == 2:
                *arrived, fields = after(*arrived, fields)
    readings = jnp.concatenate(readings, axis=0)
    goal_block, ritz_gram = readings_exchange(readings, sensor_owner, sensor_count, goal_weight)
    return fields, goal_block, ritz_gram


def solution(mesh):
    torus = Mesh(mesh.devices.reshape(4, 4, 2, mesh.shape["gy"]), ALL)
    return jax.shard_map(
        body,
        mesh=torus,
        in_specs=(
            P(None, GX, "gy", None),
            P(GX, "gy", None),
            P(),
            P(GX, "gy", None),
            P(GX, "gy", None, None),
            P(GX, "gy"),
            P(GX, "gy", None, None),
        ),
        out_specs=(P(None, GX, "gy", None), P(ALL, None), P()),
        check_vma=False,
    )
```
